32 devices in a mesh: dp: 4 (over y, x), fsdp: 8 (over z, core).
Axes of the slice: x: 2, y: 2, z: 4, core: 2. Of those that a mesh axis runs over, the one named last changes fastest.
Arguments:
- tokens: bfloat16 [12288, 8192], P(('dp', 'fsdp')), may hold values from -6 to 6
- frozen_value_weight: bfloat16 [8192, 1024], P('fsdp'), may hold values from -0.0625 to 0.0625
- adapter_down_weight: bfloat16 [32, 8192, 64], P('dp', 'fsdp'), may hold values from -0.0625 to 0.0625
- adapter_up_weight: bfloat16 [32, 64, 1024], P('dp', None, 'fsdp'), may hold values from -0.75 to 0.75
- output_gradient: bfloat16 [12288, 1024], P(('dp', 'fsdp')), may hold values from -6 to 6
- adapter_per_block: int32 [96], P(('dp', 'fsdp')), may hold values from 0 to 31, as said below
- block_live_count: int32 [96], P(('dp', 'fsdp')), may hold values from 1 to 128
Outputs:
- values: bfloat16 [12288, 1024], P(('dp', 'fsdp'))
- input_gradient: bfloat16 [12288, 8192], P(('dp', 'fsdp'))
- grad_down: float32 [32, 8192, 64], P('dp', 'fsdp')
- grad_up: float32 [32, 64, 1024], P('dp', None, 'fsdp')
The draws below stay inside these ranges and needn't reach their ends.
Inputs may be any that keep to these rules, and one draw needn't show every extreme that they name: `adapter_per_block`: within the blocks of one device the adapter numbers never fall.
All inputs are finite; a program needn't handle non-finite values.
Results may differ from the reference program's by a relative error of at most 0.0038.
Values may be sent and summed in bfloat16 or wider, within the bound.
A program may use at most 192 MiB of HBM per device.

```python
import jax
import jax.numpy as jnp
from jax import lax

MODEL_WIDTH = 8192
VALUE_WIDTH = 1024
ADAPTER_RANK = 64
ADAPTER_COUNT = 32
BLOCK = 128
TOK_DEV = 384
TOKEN_SLOTS = 12288
N_BLOCKS = 96


def draw_adapter_per_block(key, part):
    per_dev = TOK_DEV // BLOCK
    groups = N_BLOCKS // per_dev
    upper_key, number_key, place_key = jax.random.split(jax.random.fold_in(key, 7), 3)
    upper = jax.random.randint(upper_key, (N_BLOCKS,), 1, ADAPTER_COUNT + 1)
    numbers = jax.random.randint(number_key, (N_BLOCKS,), 0, upper)
    ordered = jnp.sort(numbers.reshape(groups, per_dev), axis=1)
    ordered = ordered.at[0, 0].set(0)
    chosen = jax.random.randint(place_key, (), 1, groups)
    ordered = ordered.at[chosen, per_dev - 1].set(ADAPTER_COUNT - 1)
    return ordered.reshape(N_BLOCKS).astype(jnp.int32)


def set_ends(drawn, key, low, top_value):
    place = [jax.random.randint(jax.random.fold_in(key, axis), (), 0, length) for axis, length in enumerate(drawn.shape)]
    main_axis = drawn.shape.index(max(drawn.shape))
    beside = place[:main_axis] + [(place[main_axis] + 1) % drawn.shape[main_axis]] + place[main_axis + 1:]
    return drawn.at[tuple(place)].set(low).at[tuple(beside)].set(top_value)


def steps_of(own_key, shape, shards, low, top_value):
    loudness, own = 1.0, jax.random.fold_in(own_key, 6)
    for position, parts in shards:
        heights = jnp.exp(jax.random.uniform(jax.random.fold_in(own, position), (parts,), jnp.float32, low / len(shards), top_value / len(shards)))
        loudness = loudness * jnp.repeat(heights, shape[position] // parts).reshape([-1 if axis == position else 1 for axis in range(len(shape))])
    return loudness


def centred(rng, shape, spread, limit, shards=(), kind=jnp.bfloat16):
    drawn = jax.random.normal(rng, shape, jnp.float32) * spread
    if len(shards) > 0:
        drawn = steps_of(rng, shape, shards, -0.22, 0.18) * drawn
    return jnp.clip(drawn, min=-limit, max=limit).astype(kind)


def setup_inputs(seed: int = 0) -> dict:
    arg_keys = jax.random.split(jax.random.key(seed), 8)
    tokens = centred(arg_keys[0], (TOKEN_SLOTS, MODEL_WIDTH), 1.0, 6.0, ((0, 32),))
    frozen_value_weight = centred(arg_keys[1], (MODEL_WIDTH, VALUE_WIDTH), MODEL_WIDTH ** -0.5, 0.0625, ((0, 8),))
    adapter_down_weight = centred(arg_keys[2], (ADAPTER_COUNT, MODEL_WIDTH, ADAPTER_RANK), MODEL_WIDTH ** -0.5, 0.0625, ((0, 4), (1, 8)))
    adapter_up_weight = centred(arg_keys[3], (ADAPTER_COUNT, ADAPTER_RANK, VALUE_WIDTH), ADAPTER_RANK ** -0.5, 0.75, ((0, 4), (2, 8)))
    output_gradient = centred(arg_keys[4], (TOKEN_SLOTS, VALUE_WIDTH), 1.0, 6.0, ((0, 32),))
    adapter_per_block = draw_adapter_per_block(jax.random.fold_in(arg_keys[7], 71), 0)
    block_live_count = set_ends(jax.random.randint(arg_keys[6], (N_BLOCKS,), 1, BLOCK + 1), jax.random.fold_in(arg_keys[6], 1), 1, BLOCK).astype(jnp.int32)
    return {"tokens": tokens, "frozen_value_weight": frozen_value_weight, "adapter_down_weight": adapter_down_weight, "adapter_up_weight": adapter_up_weight, "output_gradient": output_gradient, "adapter_per_block": adapter_per_block, "block_live_count": block_live_count}


adapter_scale = 0.5


def reference(tokens, frozen_value_weight, adapter_down_weight, adapter_up_weight, output_gradient, adapter_per_block, block_live_count):
    frozen_output = jnp.dot(tokens, frozen_value_weight, preferred_element_type=jnp.float32)
    frozen_gradient = lax.dot_general(output_gradient, frozen_value_weight, (((1,), (1,)), ((), ())), preferred_element_type=jnp.float32)
    per_dev = TOK_DEV // BLOCK
    groups = N_BLOCKS // per_dev
    input_per_block = tokens.reshape(groups, per_dev, BLOCK, MODEL_WIDTH)
    dy_blocks = output_gradient.reshape(groups, per_dev, BLOCK, VALUE_WIDTH)
    ids = adapter_per_block.reshape(groups, per_dev)
    fills = block_live_count.reshape(groups, per_dev)
    positions = jnp.arange(BLOCK, dtype=jnp.int32)
    catalog = jnp.arange(ADAPTER_COUNT, dtype=jnp.int32)

    def one_device(carry, inputs):
        down_gradient_sum, up_gradient_sum = carry
        x_dev, dy_dev, adapter_index_local, fill_dev = inputs
        live_slot_mask = (positions[None, :] < fill_dev[:, None]).astype(jnp.float32)[:, :, None]
        down_per_block = adapter_down_weight[adapter_index_local].astype(jnp.float32)
        up_per_block = adapter_up_weight[adapter_index_local].astype(jnp.float32)
        input_gathered = x_dev.astype(jnp.float32)
        dy_wide = dy_dev.astype(jnp.float32)
        reduced_down_output = (jnp.einsum('gzq,gqx->gzx', input_gathered, down_per_block) * live_slot_mask).astype(jnp.bfloat16)
        reduced_output_gradient = (jnp.einsum('bkc,brc->bkr', dy_wide, up_per_block) * live_slot_mask).astype(jnp.bfloat16)
        raised_rows = jnp.einsum('bkr,brc->bkc', reduced_down_output.astype(jnp.float32), up_per_block).astype(jnp.bfloat16)
        collected_rows = jnp.einsum('qjz,qaz->qja', reduced_output_gradient.astype(jnp.float32), down_per_block).astype(jnp.bfloat16)
        choose = (adapter_index_local[:, None] == catalog[None, :]).astype(jnp.float32)
        up_terms = jnp.einsum('bkr,bkc->brc', reduced_down_output.astype(jnp.float32), dy_wide)
        down_gradient_terms = jnp.einsum('uia,uiw->uaw', input_gathered, reduced_output_gradient.astype(jnp.float32))
        down_gradient_sum = down_gradient_sum + jnp.einsum('ba,bdr->adr', choose, down_gradient_terms, precision=lax.Precision.HIGHEST)
        up_gradient_sum = up_gradient_sum + jnp.einsum('ba,brc->arc', choose, up_terms, precision=lax.Precision.HIGHEST)
        return (down_gradient_sum, up_gradient_sum), (raised_rows, collected_rows)

    start = (jnp.zeros((ADAPTER_COUNT, MODEL_WIDTH, ADAPTER_RANK), jnp.float32), jnp.zeros((ADAPTER_COUNT, ADAPTER_RANK, VALUE_WIDTH), jnp.float32))
    (down_gradient_sum, up_gradient_sum), (raised_rows, collected_rows) = lax.scan(one_device, start, (input_per_block, dy_blocks, ids, fills))
    values = (frozen_output + adapter_scale * raised_rows.reshape(TOKEN_SLOTS, VALUE_WIDTH).astype(jnp.float32)).astype(jnp.bfloat16)
    input_gradient = (frozen_gradient + adapter_scale * collected_rows.reshape(TOKEN_SLOTS, MODEL_WIDTH).astype(jnp.float32)).astype(jnp.bfloat16)
    return values, input_gradient, adapter_scale * down_gradient_sum, adapter_scale * up_gradient_sum
```

```python
import jax
import jax.numpy as jnp
from jax import lax
from jax.experimental import pallas as pl
from jax.experimental.pallas import tpu as pltpu
from jax.sharding import PartitionSpec as P

adapter_scale = 0.5
cores = 2


def spread(part, axis):
    size = lax.axis_size(axis)
    copies = jnp.broadcast_to(part[None], (size,) + part.shape)
    return lax.all_to_all(copies, axis, split_axis=0, concat_axis=0, tiled=True)


def gather_frozen(piece, first, second):
    dp, fsdp = lax.axis_size("dp"), lax.axis_size("fsdp")
    rows, width = piece.shape
    chips = fsdp // cores
    share_rows = rows // dp
    share = lax.dynamic_slice_in_dim(piece, lax.axis_index("dp") * share_rows, share_rows, 0)
    same_core = [[chip * cores + core for chip in range(chips)] for core in range(cores)]
    same_chip = [[chip * cores + core for core in range(cores)] for chip in range(chips)]
    shares = lax.all_gather(share, "fsdp", axis=0, axis_index_groups=same_core)
    shares, _ = lax.optimization_barrier((shares, first))
    half = lax.all_gather(shares, "dp", axis=0)
    half, _ = lax.optimization_barrier((half, second))
    return lax.all_gather(half, "fsdp", axis=0, axis_index_groups=same_chip)


def dot(left, right, left_dim, right_dim):
    return lax.dot_general(
        left, right, (((left_dim,), (right_dim,)), ((), ())), preferred_element_type=jnp.float32
    )


def low_rank_kernel(fill_ref, x_ref, dy_ref, pieces_ref, terms_ref, u_ref, v_ref, u_sum, v_sum):
    slices, per_dev, rank, _ = pieces_ref.shape
    block_rows, outputs = dy_ref.shape[2:]
    features = x_ref.shape[1] // slices
    u_sum[...] = jnp.zeros_like(u_sum)
    v_sum[...] = jnp.zeros_like(v_sum)

    def x_of(block, index):
        columns = pl.ds(pl.multiple_of(index * features, features), features)
        return x_ref[block * block_rows : (block + 1) * block_rows, columns]

    @pl.loop(0, slices)
    def _(index):
        for block in range(per_dev):
            u_sum[block] += dot(x_of(block, index), pieces_ref[index, block, :, :features], 1, 1)
            v_sum[block] += dot(dy_ref[index, block], pieces_ref[index, block, :, features:], 1, 1)

    rows = lax.broadcasted_iota(jnp.int32, (block_rows, rank), 0)
    for block in range(per_dev):
        live = (rows < fill_ref[block]).astype(jnp.float32)
        u_ref[block] = (u_sum[block] * live).astype(jnp.bfloat16)
        v_ref[block] = (v_sum[block] * live).astype(jnp.bfloat16)

    @pl.loop(0, slices)
    def _(index):
        for block in range(per_dev):
            down_term = dot(v_ref[block], x_of(block, index), 0, 0)
            up_term = dot(u_ref[block], dy_ref[index, block], 0, 0)
            terms_ref[index, block, :, :features] = down_term.astype(jnp.bfloat16)
            terms_ref[index, block, :, features:] = up_term.astype(jnp.bfloat16)


def low_rank(fill, x, dy, pieces):
    slices, per_dev, rank, _ = pieces.shape
    block_rows = x.shape[0] // per_dev
    low = jax.ShapeDtypeStruct((per_dev, block_rows, rank), jnp.bfloat16)
    vmem = pl.BlockSpec(memory_space=pltpu.VMEM)
    size = 2 * (x.size + dy.size + 2 * pieces.size)
    return pl.pallas_call(
        low_rank_kernel,
        out_shape=(jax.ShapeDtypeStruct(pieces.shape, jnp.bfloat16), low, low),
        in_specs=[pl.BlockSpec(memory_space=pltpu.SMEM), vmem, vmem, vmem],
        out_specs=(vmem, vmem, vmem),
        scratch_shapes=[pltpu.VMEM(low.shape, jnp.float32)] * 2,
        cost_estimate=pl.CostEstimate(
            flops=8 * x.size * rank, bytes_accessed=size, transcendentals=0
        ),
        name="low_rank",
    )(fill, x, dy, pieces)


def combine_kernel(ids_ref, terms_ref, out_ref, total):
    total[...] = jnp.zeros_like(total)

    @pl.loop(0, terms_ref.shape[0])
    def _(block):
        owner = ids_ref[block]
        total[owner] += terms_ref[block].astype(jnp.float32)

    out_ref[...] = total[...].astype(out_ref.dtype)


def combine(ids, terms, adapters):
    shape = (adapters,) + terms.shape[1:]
    vmem = pl.BlockSpec(memory_space=pltpu.VMEM)
    return pl.pallas_call(
        combine_kernel,
        out_shape=jax.ShapeDtypeStruct(shape, jnp.bfloat16),
        in_specs=[pl.BlockSpec(memory_space=pltpu.SMEM), vmem],
        out_specs=vmem,
        scratch_shapes=[pltpu.VMEM(shape, jnp.float32)],
        name="combine",
    )(ids, terms)


def base_kernel(x_ref, dy_ref, w_ref, pieces_ref, up_ref, u_ref, v_ref, y_ref, dx_ref, total):
    index = pl.program_id(0)
    per_dev, block_rows, _ = u_ref.shape
    features = x_ref.shape[1]
    frozen = w_ref[...].reshape(features, w_ref.shape[-1])
    product = dot(x_ref[...], frozen, 1, 0)

    @pl.when(index == 0)
    def _():
        total[...] = product

    @pl.when(index > 0)
    def _():
        total[...] += product

    base_grad = dot(dy_ref[...], frozen, 1, 1)
    for block in range(per_dev):
        rows = slice(block * block_rows, (block + 1) * block_rows)
        pulled = dot(v_ref[block], pieces_ref[0, block, :, :features], 1, 0)
        pulled = pulled.astype(jnp.bfloat16).astype(jnp.float32)
        dx_ref[rows, :] = (base_grad[rows, :] + adapter_scale * pulled).astype(dx_ref.dtype)

    @pl.when(index == pl.num_programs(0) - 1)
    def _():
        for block in range(per_dev):
            rows = slice(block * block_rows, (block + 1) * block_rows)
            lifted = dot(u_ref[block], up_ref[block], 1, 0)
            lifted = lifted.astype(jnp.bfloat16).astype(jnp.float32)
            y_ref[rows, :] = (total[rows, :] + adapter_scale * lifted).astype(y_ref.dtype)


def base(x, dy, gathered, pieces, up, low_u, low_v):
    slices, per_dev, rank, piece_width = pieces.shape
    count_dev, model_width = x.shape
    width = dy.shape[1]
    features = model_width // slices
    _, dp, _, share_rows, _ = gathered.shape

    def whole(array):
        return pl.BlockSpec(array.shape, lambda index: (0,) * array.ndim)

    tile = pl.BlockSpec((count_dev, features), lambda index: (0, index))
    return pl.pallas_call(
        base_kernel,
        grid=(slices,),
        out_shape=(
            jax.ShapeDtypeStruct(dy.shape, jnp.bfloat16),
            jax.ShapeDtypeStruct(x.shape, jnp.bfloat16),
        ),
        in_specs=[
            tile,
            whole(dy),
            pl.BlockSpec(
                (1, dp, 1, share_rows, width),
                lambda index: (index % cores, 0, index // cores, 0, 0),
            ),
            pl.BlockSpec((1, per_dev, rank, piece_width), lambda index: (index, 0, 0, 0)),
            whole(up),
            whole(low_u),
            whole(low_v),
        ],
        out_specs=(whole(dy), tile),
        scratch_shapes=[pltpu.VMEM(dy.shape, jnp.float32)],
        compiler_params=pltpu.CompilerParams(dimension_semantics=("arbitrary",)),
        cost_estimate=pl.CostEstimate(
            flops=4 * x.size * width,
            bytes_accessed=2 * (2 * x.size + model_width * width),
            transcendentals=0,
        ),
        name="base",
    )(x, dy, gathered, pieces, up, low_u, low_v)


def body(
    tokens,
    frozen_value_weight,
    adapter_down_weight,
    adapter_up_weight,
    output_gradient,
    adapter_per_block,
    block_live_count,
):
    dp, fsdp = lax.axis_size("dp"), lax.axis_size("fsdp")
    count_dev, model_width = tokens.shape
    value_width = output_gradient.shape[1]
    per_dev = adapter_per_block.shape[0]
    block_rows = count_dev // per_dev
    own, features, rank = adapter_down_weight.shape
    outputs = adapter_up_weight.shape[2]
    total = own * dp
    ids_all = lax.all_gather(adapter_per_block, "fsdp", axis=0, tiled=True)
    ids_all, down, up = lax.optimization_barrier(
        (ids_all, adapter_down_weight, adapter_up_weight)
    )
    pieces = jnp.concatenate([down.transpose(0, 2, 1), up], axis=2)
    catalog_pieces = spread(pieces, "dp").reshape(total, rank, features + outputs)
    chosen = catalog_pieces[ids_all].reshape(fsdp, per_dev, rank, features + outputs)
    arrived = lax.all_to_all(chosen, "fsdp", split_axis=0, concat_axis=0, tiled=True)
    up_blocks = arrived[..., features:].transpose(1, 2, 0, 3).reshape(per_dev, rank, value_width)
    dy_slices = output_gradient.reshape(per_dev, block_rows, fsdp, outputs).transpose(2, 0, 1, 3)
    terms, low_u, low_v = low_rank(block_live_count, tokens, dy_slices, arrived)
    terms = lax.all_to_all(terms, "fsdp", split_axis=0, concat_axis=0, tiled=True)
    terms = terms.reshape(fsdp * per_dev, rank, features + outputs)
    sums = combine(ids_all, terms, total).reshape(dp, own, rank, features + outputs)
    sums = lax.all_to_all(sums, "dp", split_axis=0, concat_axis=0, tiled=True)
    gathered = gather_frozen(frozen_value_weight, catalog_pieces, terms)
    values, input_gradient = base(
        tokens, output_gradient, gathered, arrived, up_blocks, low_u, low_v
    )
    sums, values, input_gradient = lax.optimization_barrier((sums, values, input_gradient))
    gradients = adapter_scale * jnp.sum(sums.astype(jnp.float32), axis=0)
    grad_down = gradients[..., :features].transpose(0, 2, 1)
    grad_up = gradients[..., features:]
    return values, input_gradient, grad_down, grad_up


def solution(mesh):
    placed = (
        P(("dp", "fsdp"), None),
        P("fsdp", None),
        P("dp", "fsdp", None),
        P("dp", None, "fsdp"),
        P(("dp", "fsdp"), None),
        P(("dp", "fsdp")),
        P(("dp", "fsdp")),
    )
    return jax.shard_map(
        body,
        mesh=mesh,
        in_specs=placed,
        out_specs=(
            P(("dp", "fsdp"), None),
            P(("dp", "fsdp"), None),
            P("dp", "fsdp", None),
            P("dp", None, "fsdp"),
        ),
        check_vma=False,
    )
```
